256 devices in a mesh: half: 2 (over y_hi), row: 16 (over z, y_lo), col: 8 (over x, core).
Axes of the slice: x: 4, y: 4 (y_hi: 2, y_lo: 2; y = y_hi * 2 + y_lo), z: 8, core: 2. Of those that a mesh axis runs over, the one named last changes fastest.
Arguments:
- children: bfloat16 [2, 512, 512, 512], P('half', 'row', 'col'), may hold values from -0.01171875 to 0.01171875
- operators: bfloat16 [2, 2, 4, 512, 512], P('half'), may hold values from -1 to 1
- term_site: int32 [2, 5, 2], P('half'), may hold values from 0 to 3
- term_leg: int32 [2, 5], P('half'), may hold values from 0 to 2
- parent: bfloat16 [512, 512, 512], P(('half', 'row', 'col')), may hold values from -6 to 6
Outputs:
- updated: bfloat16 [512, 512, 512], P(('half', 'row', 'col'))
The draws below stay inside these ranges and needn't reach their ends.
Inputs may be any that keep to these rules, and one draw needn't show every extreme that they name: `term_site`: a site index into the child's operator table of 4 entries. `term_leg`: 0: the term acts on the first leg only, 1: on the second leg only, 2: on both.
All inputs are finite; a program needn't handle non-finite values.
Results may differ from the reference program's by a relative error of at most 0.0064.
Values may be sent and summed in bfloat16 or wider, within the bound.
No kernel may reach another device: no remote copies, remote signals or barrier semaphores. Data moves between devices by JAX's collectives and lax.ppermute only.
A program may use at most 128 MiB of HBM per device.

```python
import jax
import jax.numpy as jnp
from jax import lax

B = 512
C = 512
TERMS = 5
SITES = 4


def touch_ends(entries, stream_key, least, high):
    longest = entries.shape.index(max(entries.shape))
    spots = []
    for shift in (0, 1):
        where = [jax.random.randint(jax.random.fold_in(stream_key, axis), (), 0, length) for axis, length in enumerate(entries.shape)]
        where[longest] = (where[longest] + shift) % entries.shape[longest]
        spots.append(tuple(where))
    return entries.at[spots[0]].set(least).at[spots[1]].set(high)


def block_levels(own_key, dims, cuts, least, top_value):
    gain = 1.0
    for dim, parts in cuts:
        draws = jax.random.uniform(jax.random.fold_in(jax.random.fold_in(own_key, 6), dim), (parts,), jnp.float32, least / len(cuts), top_value / len(cuts))
        gain = gain * jnp.repeat(jnp.exp(draws), dims[dim] // parts).reshape((-1,) + (1,) * (len(dims) - 1 - dim))
    return gain


def scatter_about(rng, shape, deviation, most, cuts=(), kind=jnp.bfloat16):
    array = jax.random.normal(rng, shape, jnp.float32) * deviation
    if len(cuts) > 0:
        array = block_levels(rng, shape, cuts, -0.22, 0.18) * array
    return jnp.clip(array, min=-most, max=most).astype(kind)


def setup_inputs(seed: int = 0) -> dict:
    splits = jax.random.split(jax.random.key(seed), 6)
    return {
        "children": scatter_about(splits[0], (2, B, B, B), (B * B) ** -0.5, 0.01171875, ((0, 2), (1, 16), (2, 8))),
        "operators": scatter_about(splits[1], (2, 2, SITES, B, B), (B // 16) ** -0.5, 1.0, ((0, 2),)),
        "term_site": touch_ends(jax.random.randint(splits[2], (2, TERMS, 2), 0, SITES), jax.random.fold_in(splits[2], 1), 0, SITES - 1).astype(jnp.int32),
        "term_leg": touch_ends(jax.random.randint(splits[3], (2, TERMS), 0, 3), jax.random.fold_in(splits[3], 1), 0, 2).astype(jnp.int32),
        "parent": scatter_about(splits[4], (C, B, B), 1.0, 6.0, ((0, 256),)),
    }


def apply_terms(block, table, site_ids, leg_codes):
    identity = jnp.eye(B, dtype=block.dtype)
    accumulated = jnp.zeros(block.shape, jnp.float32)
    for term in range(TERMS):
        left_op = jnp.where(leg_codes[term] != 1, table[0, site_ids[term, 0]], identity)
        right_op = jnp.where(leg_codes[term] != 0, table[1, site_ids[term, 1]], identity)
        inner = jnp.einsum('aik,jk->aij', block.astype(jnp.float32), right_op.astype(jnp.float32)).astype(jnp.bfloat16)
        accumulated = accumulated + jnp.einsum('ik,akj->aij', left_op.astype(jnp.float32), inner.astype(jnp.float32))
    return accumulated.astype(jnp.bfloat16)


def environment_of(child, table, site_ids, leg_codes):
    group = min(64, B)
    blocks = child.reshape(B // group, group, B, B)
    summed = lax.map(lambda piece: apply_terms(piece, table, site_ids, leg_codes), blocks)
    flat_child = child.reshape(B, B * B)
    flat_summed = summed.reshape(B, B * B)
    product = lax.dot_general(flat_child, flat_summed, (((1,), (1,)), ((), ())), preferred_element_type=jnp.float32)
    return product.astype(jnp.bfloat16)


def reference(children, operators, term_site, term_leg, parent):
    left_env = environment_of(children[0], operators[0], term_site[0], term_leg[0])
    right_env = environment_of(children[1], operators[1], term_site[1], term_leg[1])
    parent_wide = parent.astype(jnp.float32)
    first = jnp.einsum('ak,ckb->cab', left_env.astype(jnp.float32), parent_wide)
    second = jnp.einsum('bk,cak->cab', right_env.astype(jnp.float32), parent_wide)
    return (first + second).astype(jnp.bfloat16)
```

```python
import jax
import jax.numpy as jnp
from jax import lax
from jax.experimental import pallas as pl
from jax.experimental.pallas import tpu as pltpu
from jax.sharding import Mesh
from jax.sharding import PartitionSpec as P

BF = jnp.bfloat16
F32 = jnp.float32
NZ, NY, NX, NE = 8, 2, 4, 2
COL = ("x", "e")
ROW = ("z", "y")
ROW_COL = ROW + COL
ALL = ("half",) + ROW_COL
VMEM = pl.BlockSpec(memory_space=pltpu.VMEM)
SMEM = pl.BlockSpec(memory_space=pltpu.SMEM)
LIMIT = pltpu.CompilerParams(vmem_limit_bytes=50 << 20)


def dot(a, b, ca, cb):
    return lax.dot_general(a, b, (((ca,), (cb,)), ((), ())), preferred_element_type=F32)


def swap(value, axes, offset):
    peers = lax.axis_size(axes)
    return lax.ppermute(value, axes, [(i, i ^ offset) for i in range(peers)])


def terms_kernel(me, site, leg, table, *refs):
    blocks, (out_ref, whole, inner, acc) = refs[: NX * NE], refs[NX * NE :]
    col = me[1] * NE + me[0]
    rows = whole.shape[0]
    for k, ref in enumerate(blocks):
        for a in range(rows):
            whole[a, col ^ k] = ref[a]

    def x_of(a):
        return whole[a].reshape(512, 512)

    for term in range(leg.shape[0]):
        code = leg[term]

        @pl.when(code != 0)
        def _():
            right = table[1, site[term, 1]]
            for a in range(rows):
                inner[a] = dot(x_of(a), right, 1, 1).astype(BF)

        @pl.when(code == 0)
        def _():
            for a in range(rows):
                inner[a] = x_of(a)

        @pl.when(code != 1)
        def _():
            left = table[0, site[term, 0]]
            for a in range(rows):
                part = dot(left, inner[a], 1, 0)
                acc[a] = part if term == 0 else acc[a] + part

        @pl.when(code == 1)
        def _():
            for a in range(rows):
                part = inner[a].astype(F32)
                acc[a] = part if term == 0 else acc[a] + part

    for a in range(rows):
        for x in range(NX):
            for e in range(NE):
                at = x * 128 + e * 64
                for y in range(NY):
                    block = acc[a, at : at + 64, y * 256 : (y + 1) * 256]
                    out_ref[:, y, x, a // 2, a % 2, e] = block.astype(BF).reshape(NZ, 8, 256)


def apply_terms(me, site, leg, table, arrived):
    return pl.pallas_call(
        terms_kernel,
        out_shape=jax.ShapeDtypeStruct((NZ, NY, NX, NE, 2, NE, 8, 256), BF),
        in_specs=[SMEM] * 3 + [VMEM] * (1 + NX * NE),
        out_specs=VMEM,
        scratch_shapes=[
            pltpu.VMEM((4, NX * NE, 64, 512), BF),
            pltpu.VMEM((4, 512, 512), BF),
            pltpu.VMEM((4, 512, 512), F32),
        ],
        compiler_params=LIMIT,
        name="terms",
    )(me, site, leg, table, *arrived)


def turn_kernel(in_ref, out_ref):
    out_ref[...] = jnp.swapaxes(in_ref[...], 0, 1)


def turned(value):
    rows, depth, lanes = value.shape
    step = 64
    return pl.pallas_call(
        turn_kernel,
        out_shape=jax.ShapeDtypeStruct((depth, rows, lanes), BF),
        grid=(rows // step,),
        in_specs=[pl.BlockSpec((step, depth, lanes), lambda i: (i, 0, 0))],
        out_specs=pl.BlockSpec((depth, step, lanes), lambda i: (0, i, 0)),
        compiler_params=LIMIT,
        name="turn",
    )(value)


def gram_kernel(me, s_ref, own_ref, other_ref, out_ref, acc):
    e = me[0]
    first = True
    for which, c_ref in enumerate((own_ref, other_ref)):
        block = s_ref[:, :, e if which == 0 else 1 - e]
        block = jnp.swapaxes(block.reshape(256, 8, 256), 0, 1)
        for s in range(8):
            part = dot(block[s], c_ref[s], 1, 1)
            acc[...] = part if first else acc[...] + part
            first = False
    for z in range(NZ):
        for x in range(NX):
            at = (z * NX + x) * 8
            for y in range(NY):
                out_ref[z, y, x] = acc[at : at + 8, y * 256 : (y + 1) * 256].astype(BF)


def gram(me, summed, own, other):
    return pl.pallas_call(
        gram_kernel,
        out_shape=jax.ShapeDtypeStruct((NZ, NY, NX, 8, 256), BF),
        in_specs=[SMEM, VMEM, VMEM, VMEM],
        out_specs=VMEM,
        scratch_shapes=[pltpu.VMEM((256, 512), F32)],
        compiler_params=LIMIT,
        name="gram",
    )(me, summed, own, other)


def final_kernel(me, rows_ref, cols_ref, *refs):
    pieces, (out_ref, env, acc) = refs[: NX * NE], refs[-3:]
    e, x = me[0], me[1]
    for i, ref in enumerate(pieces):
        ke, kx = i % NE, i // NE
        block = (e ^ ke) * 32 + (x ^ kx)
        for half in range(2):
            for z in range(NZ):
                for y in range(NY):
                    env[half, y, block + z * NX] = ref[(half * NZ + z) * NY + y]
    for part in range(2):
        at = slice(part * 256, part * 256 + 256)
        one = env[0, part].reshape(512, 256)
        for c in range(2):
            acc[c, at, :] = dot(one, rows_ref[c], 0, 0)
    for part in range(2):
        at = slice(part * 256, part * 256 + 256)
        two = env[1, part].reshape(512, 256)
        for c in range(2):
            out_ref[c, :, at] = (acc[c, :, at] + dot(cols_ref[c], two, 1, 0)).astype(BF)


def final(me, by_rows, by_cols, pieces):
    return pl.pallas_call(
        final_kernel,
        out_shape=jax.ShapeDtypeStruct((2, 512, 512), BF),
        in_specs=[SMEM] + [VMEM] * (2 + NX * NE),
        out_specs=VMEM,
        scratch_shapes=[
            pltpu.VMEM((2, NY, 64, 8, 256), BF),
            pltpu.VMEM((2, 512, 512), F32),
        ],
        compiler_params=LIMIT,
        name="final",
    )(me, by_rows, by_cols, *pieces)


def reordered(parent):
    wanted = jnp.arange(512).reshape(128, NE, 2).swapaxes(0, 1).reshape(512)
    pick = (jnp.arange(512)[:, None] == wanted[None, :]).astype(BF)
    by_rows = jnp.einsum("aq,cab->cqb", pick, parent, preferred_element_type=F32)
    by_cols = jnp.einsum("cab,bq->caq", parent, pick, preferred_element_type=F32)
    return by_rows.astype(BF), by_cols.astype(BF)


def on_device(children, operators, term_site, term_leg, parent):
    me = jnp.stack([lax.axis_index(a) for a in ("e", "x")]).astype(jnp.int32)
    child = children[0]
    with jax.named_scope("child_rows"):
        cut = child.reshape(32, NZ, 8, NY, 256).transpose(1, 3, 0, 2, 4)
        cut = cut.reshape(NZ * NY, 32 * 8, 256)
        child_all = lax.all_to_all(cut, ROW, 0, 0, tiled=True)
    with jax.named_scope("child_first_leg"):
        col = lax.axis_index(COL)
        blocks = child.reshape(NX * NE, 4, 64, 512)
        arrived = []
        for k in range(NX * NE):
            block = lax.dynamic_index_in_dim(blocks, col ^ k, 0, keepdims=False)
            arrived.append(swap(block, COL, k) if k else block)
    with jax.named_scope("terms"):
        summed = apply_terms(
            me, term_site[0], term_leg[0], operators[0], arrived
        )
    with jax.named_scope("summed_rows"):
        summed = lax.all_to_all(summed.reshape(128, 32, 256), ROW_COL, 0, 0, tiled=True)
    with jax.named_scope("turn"):
        own = turned(child_all.reshape(512, 8, 256))
        other = swap(own, ("e",), 1)
        by_rows, by_cols = reordered(parent)
    with jax.named_scope("gram"):
        part = gram(me, summed.reshape(128, 2, NE, 8, 256), own, other)
    with jax.named_scope("sum"):
        parts = lax.all_to_all(part.reshape(64, 8, 256), ("z", "y", "x"), 0, 0, tiled=True)
        env = jnp.sum(parts.astype(F32), axis=0).astype(BF)
    with jax.named_scope("gather_row"):
        env = jnp.broadcast_to(env, (2 * NZ * NY, 8, 256))
        env = lax.all_to_all(env, ("half",) + ROW, 0, 0, tiled=True)
    with jax.named_scope("gather_x"):
        across = [env] + [swap(env, ("x",), k) for k in range(1, NX)]
    with jax.named_scope("gather_e"):
        pieces = []
        for piece in across:
            pieces += [piece, swap(piece, ("e",), 1)]
    with jax.named_scope("final"):
        return final(me, by_rows, by_cols, pieces)


def solution(mesh):
    torus = Mesh(
        mesh.devices.reshape(2, NZ, NY, NX, NE), ("half", "z", "y", "x", "e")
    )
    in_specs = (
        P("half", ROW, COL, None),
        P("half", None, None, None, None),
        P("half", None, None),
        P("half", None),
        P(ALL, None, None),
    )
    return jax.shard_map(
        on_device, mesh=torus, in_specs=in_specs, out_specs=P(ALL, None, None), check_vma=False
    )
```

```python
import jax
import jax.numpy as jnp
from jax import lax
from jax.experimental import pallas as pl
from jax.experimental.pallas import tpu as pltpu
from jax.sharding import Mesh
from jax.sharding import PartitionSpec as P

BF = jnp.bfloat16
F32 = jnp.float32
NZ, NY, NX, NE = 8, 2, 4, 2
COL = ("x", "e")
ROW = ("z", "y")
ROW_COL = ROW + COL
ALL = ("half",) + ROW_COL
VMEM = pl.BlockSpec(memory_space=pltpu.VMEM)
SMEM = pl.BlockSpec(memory_space=pltpu.SMEM)
LIMIT = pltpu.CompilerParams(vmem_limit_bytes=50 << 20)


def dot(a, b, ca, cb):
    return lax.dot_general(a, b, (((ca,), (cb,)), ((), ())), preferred_element_type=F32)


def swap(value, axes, offset):
    peers = lax.axis_size(axes)
    return lax.ppermute(value, axes, [(i, i ^ offset) for i in range(peers)])


def turn_z(value, offset):
    return lax.ppermute(value, ("z",), [(i, (i + offset) % NZ) for i in range(NZ)]) if offset else value


def terms_kernel(site, leg, table, x_ref, out_ref, inner, acc):
    rows = x_ref.shape[1]

    def x_of(a):
        return x_ref[:, a].reshape(512, 512)

    for term in range(leg.shape[0]):
        code = leg[term]

        @pl.when(code != 0)
        def _():
            right = table[1, site[term, 1]]
            for a in range(rows):
                inner[a] = dot(x_of(a), right, 1, 1).astype(BF)

        @pl.when(code == 0)
        def _():
            for a in range(rows):
                inner[a] = x_of(a)

        @pl.when(code != 1)
        def _():
            left = table[0, site[term, 0]]
            for a in range(rows):
                part = dot(left, inner[a], 1, 0)
                acc[a] = part if term == 0 else acc[a] + part

        @pl.when(code == 1)
        def _():
            for a in range(rows):
                part = inner[a].astype(F32)
                acc[a] = part if term == 0 else acc[a] + part

    for a in range(rows):
        for x in range(NX):
            for e in range(NE):
                at = x * 128 + e * 64
                for y in range(NY):
                    block = acc[a, at : at + 64, y * 256 : (y + 1) * 256]
                    out_ref[:, y, x, a // 2, a % 2, e] = block.astype(BF).reshape(NZ, 8, 256)


def apply_terms(site, leg, table, arrived):
    return pl.pallas_call(
        terms_kernel,
        out_shape=jax.ShapeDtypeStruct((NZ, NY, NX, NE, 2, NE, 8, 256), BF),
        in_specs=[SMEM, SMEM, VMEM, VMEM],
        out_specs=VMEM,
        scratch_shapes=[pltpu.VMEM((4, 512, 512), BF), pltpu.VMEM((4, 512, 512), F32)],
        compiler_params=LIMIT,
        cost_estimate=pl.CostEstimate(flops=8 * 5 * 2 * 512**3, transcendentals=0, bytes_accessed=8 << 20),
        name="terms",
    )(site, leg, table, arrived)


SHIFTS = (4, 3, 5, 2, 6, 1, 7, 0)


def turn_kernel(me, *refs):
    blocks, out_ref = refs[:-1], refs[-1]
    z, y = me[2], me[3]
    for i, ref in enumerate(blocks):
        source = lax.rem(z + NZ - SHIFTS[i % NZ], NZ) * NY + (y ^ (i // NZ))
        out_ref[:, pl.ds(pl.multiple_of(source * 32, 32), 32), :] = jnp.swapaxes(ref[...], 0, 1)


def turned(me, blocks):
    return pl.pallas_call(
        turn_kernel,
        out_shape=jax.ShapeDtypeStruct((8, 512, 256), BF),
        in_specs=[SMEM] + [VMEM] * len(blocks),
        out_specs=VMEM,
        compiler_params=LIMIT,
        name="turn",
    )(me, *blocks)


def gram_kernel(me, s_ref, own_ref, other_ref, out_ref, acc):
    e = me[0]
    first = True
    for which, c_ref in enumerate((own_ref, other_ref)):
        block = s_ref[:, :, e if which == 0 else 1 - e]
        block = jnp.swapaxes(block.reshape(256, 8, 256), 0, 1)
        for s in range(8):
            part = dot(block[s], c_ref[s], 1, 1)
            acc[...] = part if first else acc[...] + part
            first = False
    for z in range(NZ):
        for x in range(NX):
            at = (z * NX + x) * 8
            for y in range(NY):
                out_ref[z, y, x] = acc[at : at + 8, y * 256 : (y + 1) * 256].astype(BF)


def gram(me, summed, own, other):
    return pl.pallas_call(
        gram_kernel,
        out_shape=jax.ShapeDtypeStruct((NZ, NY, NX, 8, 256), BF),
        in_specs=[SMEM, VMEM, VMEM, VMEM],
        out_specs=VMEM,
        scratch_shapes=[pltpu.VMEM((256, 512), F32)],
        compiler_params=LIMIT,
        name="gram",
    )(me, summed, own, other)


def final_kernel(me, rows_ref, cols_ref, *refs):
    pieces, (out_ref, env, acc) = refs[: NX * NE], refs[-3:]
    e, x = me[0], me[1]
    for i, ref in enumerate(pieces):
        ke, kx = i % NE, i // NE
        block = (e ^ ke) * 32 + (x ^ kx)
        for half in range(2):
            for z in range(NZ):
                for y in range(NY):
                    env[half, y, block + z * NX] = ref[(half * NZ + z) * NY + y]
    for part in range(2):
        at = slice(part * 256, part * 256 + 256)
        one = env[0, part].reshape(512, 256)
        for c in range(2):
            acc[c, at, :] = dot(one, rows_ref[c], 0, 0)
    for part in range(2):
        at = slice(part * 256, part * 256 + 256)
        two = env[1, part].reshape(512, 256)
        for c in range(2):
            out_ref[c, :, at] = (acc[c, :, at] + dot(cols_ref[c], two, 1, 0)).astype(BF)


def final(me, by_rows, by_cols, pieces):
    return pl.pallas_call(
        final_kernel,
        out_shape=jax.ShapeDtypeStruct((2, 512, 512), BF),
        in_specs=[SMEM] + [VMEM] * (2 + NX * NE),
        out_specs=VMEM,
        scratch_shapes=[
            pltpu.VMEM((2, NY, 64, 8, 256), BF),
            pltpu.VMEM((2, 512, 512), F32),
        ],
        compiler_params=LIMIT,
        name="final",
    )(me, by_rows, by_cols, *pieces)


def reordered(parent):
    wanted = jnp.arange(512).reshape(128, NE, 2).swapaxes(0, 1).reshape(512)
    pick = (jnp.arange(512)[:, None] == wanted[None, :]).astype(BF)
    by_rows = jnp.einsum("aq,cab->cqb", pick, parent, preferred_element_type=F32)
    by_cols = jnp.einsum("cab,bq->caq", parent, pick, preferred_element_type=F32)
    return by_rows.astype(BF), by_cols.astype(BF)


def on_device(children, operators, term_site, term_leg, parent):
    me = jnp.stack([lax.axis_index(a) for a in ("e", "x", "z", "y")]).astype(jnp.int32)
    child = children[0]
    with jax.named_scope("child_first_leg"):
        whole = lax.all_to_all(child.reshape(NX * NE, 4 * 64, 512), COL, 0, 0, tiled=True)
    with jax.named_scope("child_rows"):
        z, y = lax.axis_index("z"), lax.axis_index("y")
        cut = child.reshape(32, NZ, 8, NY * 256)

        def cut_for(shift, which):
            start = (0, lax.rem(z + shift, NZ), 0, which * 256)
            return lax.dynamic_slice(cut, start, (32, 1, 8, 256)).reshape(32, 8, 256)

        near, far = [], []
        for group in (SHIFTS[:4], SHIFTS[4:]):
            held = swap(jnp.stack([cut_for(shift, y ^ 1) for shift in group]), ("y",), 1)
            near += [turn_z(cut_for(shift, y), shift) for shift in group]
            far += [turn_z(held[i], shift) for i, shift in enumerate(group)]
        blocks = near + far
    with jax.named_scope("terms"):
        summed = apply_terms(
            term_site[0], term_leg[0], operators[0], whole.reshape(NX * NE, 4, 64, 512)
        )
    with jax.named_scope("summed_rows"):
        summed, blocks = lax.optimization_barrier((summed, blocks))
        summed = lax.all_to_all(summed.reshape(128, 32, 256), ROW_COL, 0, 0, tiled=True)
    with jax.named_scope("turn"):
        own = turned(me, blocks)
        other = swap(own, ("e",), 1)
        by_rows, by_cols = reordered(parent)
    with jax.named_scope("gram"):
        part = gram(me, summed.reshape(128, 2, NE, 8, 256), own, other)
    with jax.named_scope("sum"):
        parts = lax.all_to_all(part.reshape(64, 8, 256), ("z", "y", "x"), 0, 0, tiled=True)
        env = jnp.sum(parts.astype(F32), axis=0).astype(BF)
    with jax.named_scope("gather_row"):
        env = jnp.broadcast_to(env, (2 * NZ * NY, 8, 256))
        env = lax.all_to_all(env, ("half",) + ROW, 0, 0, tiled=True)
    with jax.named_scope("gather_x"):
        across = [env] + [swap(env, ("x",), k) for k in range(1, NX)]
    with jax.named_scope("gather_e"):
        pieces = []
        for piece in across:
            pieces += [piece, swap(piece, ("e",), 1)]
    with jax.named_scope("final"):
        return final(me, by_rows, by_cols, pieces)


def solution(mesh):
    torus = Mesh(
        mesh.devices.reshape(2, NZ, NY, NX, NE), ("half", "z", "y", "x", "e")
    )
    in_specs = (
        P("half", ROW, COL, None),
        P("half", None, None, None, None),
        P("half", None, None),
        P("half", None),
        P(ALL, None, None),
    )
    return jax.shard_map(
        on_device, mesh=torus, in_specs=in_specs, out_specs=P(ALL, None, None), check_vma=False
    )
```

```python
import jax
import jax.numpy as jnp
from jax import lax
from jax.experimental import pallas as pl
from jax.experimental.pallas import tpu as pltpu
from jax.sharding import Mesh
from jax.sharding import PartitionSpec as P

BF = jnp.bfloat16
F32 = jnp.float32
NZ, NY, NX, NE = 8, 2, 4, 2
COL = ("x", "e")
ROW = ("z", "y")
ROW_COL = ROW + COL
ALL = ("half",) + ROW_COL
VMEM = pl.BlockSpec(memory_space=pltpu.VMEM)
SMEM = pl.BlockSpec(memory_space=pltpu.SMEM)
HBM = pl.BlockSpec(memory_space=pltpu.HBM)


def vmem(mebibytes):
    return pltpu.CompilerParams(vmem_limit_bytes=mebibytes << 20)


def dot(a, b, ca, cb):
    return lax.dot_general(a, b, (((ca,), (cb,)), ((), ())), preferred_element_type=F32)


def swap(value, axes, offset):
    peers = lax.axis_size(axes)
    return lax.ppermute(value, axes, [(i, i ^ offset) for i in range(peers)])


def terms_kernel(me, site, leg, table, *refs):
    blocks, (out_ref, ops, whole, inner, acc, arrived) = refs[: NX * NE], refs[NX * NE :]
    sites, terms, rows = ops.shape[1], leg.shape[0], whole.shape[0]
    fetch = [
        [pltpu.make_async_copy(table.at[w, s], ops.at[w, s], arrived.at[w, s]) for s in range(sites)]
        for w in range(2)
    ]
    for copy in fetch[1] + fetch[0]:
        copy.start()
    col = me[1] * NE + me[0]
    for k, ref in enumerate(blocks):
        for a in range(rows):
            whole[a, col ^ k] = ref[a]

    def any_term(test):
        found = test(0)
        for term in range(1, terms):
            found = found | test(term)
        return found

    @pl.when(any_term(lambda term: leg[term] == 0))
    def _():
        for a in range(rows):
            inner[sites, a] = whole[a].reshape(512, 512)

    for s in range(sites):
        fetch[1][s].wait()

        @pl.when(any_term(lambda term: (leg[term] != 0) & (site[term, 1] == s)))
        def _():
            for a in range(rows):
                inner[s, a] = dot(whole[a].reshape(512, 512), ops[1, s], 1, 1).astype(BF)

    for copy in fetch[0]:
        copy.wait()
    for term in range(terms):
        code = leg[term]
        held = jnp.where(code == 0, sites, site[term, 1])

        @pl.when(code != 1)
        def _():
            left = ops[0, site[term, 0]]
            for a in range(rows):
                part = dot(left, inner[held, a], 1, 0)
                acc[a] = part if term == 0 else acc[a] + part

        @pl.when(code == 1)
        def _():
            for a in range(rows):
                part = inner[held, a].astype(F32)
                acc[a] = part if term == 0 else acc[a] + part

    for a in range(rows):
        for x in range(NX):
            for e in range(NE):
                at = x * 128 + e * 64
                for y in range(NY):
                    block = acc[a, at : at + 64, y * 256 : (y + 1) * 256]
                    out_ref[:, y, x, a // 2, a % 2, e] = block.astype(BF).reshape(NZ, 8, 256)


def apply_terms(me, site, leg, table, arrived):
    sites = table.shape[1]
    return pl.pallas_call(
        terms_kernel,
        out_shape=jax.ShapeDtypeStruct((NZ, NY, NX, NE, 2, NE, 8, 256), BF),
        in_specs=[SMEM] * 3 + [HBM] + [VMEM] * (NX * NE),
        out_specs=VMEM,
        scratch_shapes=[
            pltpu.VMEM((2, sites, 512, 512), BF),
            pltpu.VMEM((4, NX * NE, 64, 512), BF),
            pltpu.VMEM((sites + 1, 4, 512, 512), BF),
            pltpu.VMEM((4, 512, 512), F32),
            pltpu.SemaphoreType.DMA((2, sites)),
        ],
        compiler_params=vmem(50),
        name="terms",
    )(me, site, leg, table, *arrived)


def turn_kernel(in_ref, out_ref):
    out_ref[...] = jnp.swapaxes(in_ref[...], 0, 1)


def turned(value):
    rows, depth, lanes = value.shape
    step = 64
    return pl.pallas_call(
        turn_kernel,
        out_shape=jax.ShapeDtypeStruct((depth, rows, lanes), BF),
        grid=(rows // step,),
        in_specs=[pl.BlockSpec((step, depth, lanes), lambda i: (i, 0, 0))],
        out_specs=pl.BlockSpec((depth, step, lanes), lambda i: (0, i, 0)),
        compiler_params=vmem(50),
        name="turn",
    )(value)


def gram_kernel(me, s_ref, own_ref, other_ref, out_ref, acc):
    e = me[0]
    first = True
    for which, c_ref in enumerate((own_ref, other_ref)):
        block = s_ref[:, :, e if which == 0 else 1 - e]
        block = jnp.swapaxes(block.reshape(256, 8, 256), 0, 1)
        for s in range(8):
            part = dot(block[s], c_ref[s], 1, 1)
            acc[...] = part if first else acc[...] + part
            first = False
    for z in range(NZ):
        for x in range(NX):
            at = (z * NX + x) * 8
            for y in range(NY):
                out_ref[z, y, x] = acc[at : at + 8, y * 256 : (y + 1) * 256].astype(BF)


def gram(me, summed, own, other):
    return pl.pallas_call(
        gram_kernel,
        out_shape=jax.ShapeDtypeStruct((NZ, NY, NX, 8, 256), BF),
        in_specs=[SMEM, VMEM, VMEM, VMEM],
        out_specs=VMEM,
        scratch_shapes=[pltpu.VMEM((256, 512), F32)],
        compiler_params=vmem(50),
        name="gram",
    )(me, summed, own, other)


def final_kernel(me, rows_ref, cols_ref, *refs):
    pieces, (out_ref, env, acc) = refs[: NX * NE], refs[-3:]
    e, x = me[0], me[1]
    for i, ref in enumerate(pieces):
        ke, kx = i % NE, i // NE
        block = (e ^ ke) * 32 + (x ^ kx)
        for half in range(2):
            for z in range(NZ):
                for y in range(NY):
                    env[half, y, block + z * NX] = ref[(half * NZ + z) * NY + y]
    for part in range(2):
        at = slice(part * 256, part * 256 + 256)
        one = env[0, part].reshape(512, 256)
        for c in range(2):
            acc[c, at, :] = dot(one, rows_ref[c], 0, 0)
    for part in range(2):
        at = slice(part * 256, part * 256 + 256)
        two = env[1, part].reshape(512, 256)
        for c in range(2):
            out_ref[c, :, at] = (acc[c, :, at] + dot(cols_ref[c], two, 1, 0)).astype(BF)


def final(me, by_rows, by_cols, pieces):
    return pl.pallas_call(
        final_kernel,
        out_shape=jax.ShapeDtypeStruct((2, 512, 512), BF),
        in_specs=[SMEM] + [VMEM] * (2 + NX * NE),
        out_specs=VMEM,
        scratch_shapes=[
            pltpu.VMEM((2, NY, 64, 8, 256), BF),
            pltpu.VMEM((2, 512, 512), F32),
        ],
        compiler_params=vmem(50),
        name="final",
    )(me, by_rows, by_cols, *pieces)


def reordered(parent):
    wanted = jnp.arange(512).reshape(128, NE, 2).swapaxes(0, 1).reshape(512)
    pick = (jnp.arange(512)[:, None] == wanted[None, :]).astype(BF)
    by_rows = jnp.einsum("aq,cab->cqb", pick, parent, preferred_element_type=F32)
    by_cols = jnp.einsum("cab,bq->caq", parent, pick, preferred_element_type=F32)
    return by_rows.astype(BF), by_cols.astype(BF)


def on_device(children, operators, term_site, term_leg, parent):
    me = jnp.stack([lax.axis_index(a) for a in ("e", "x")]).astype(jnp.int32)
    child = children[0]
    with jax.named_scope("child_rows"):
        cut = child.reshape(32, NZ, 8, NY, 256).transpose(1, 3, 0, 2, 4)
        cut = cut.reshape(NZ * NY, 32 * 8, 256)
        child_all = lax.all_to_all(cut, ROW, 0, 0, tiled=True)
    with jax.named_scope("child_first_leg"):
        col = lax.axis_index(COL)
        blocks = child.reshape(NX * NE, 4, 64, 512)
        arrived = []
        for k in range(NX * NE):
            block = lax.dynamic_index_in_dim(blocks, col ^ k, 0, keepdims=False)
            arrived.append(swap(block, COL, k) if k else block)
    with jax.named_scope("terms"):
        summed = apply_terms(
            me, term_site[0], term_leg[0], operators[0], arrived
        )
    with jax.named_scope("summed_rows"):
        summed = lax.all_to_all(summed.reshape(128, 32, 256), ROW_COL, 0, 0, tiled=True)
    with jax.named_scope("turn"):
        own = turned(child_all.reshape(512, 8, 256))
        other = swap(own, ("e",), 1)
        by_rows, by_cols = reordered(parent)
    with jax.named_scope("gram"):
        part = gram(me, summed.reshape(128, 2, NE, 8, 256), own, other)
    with jax.named_scope("sum"):
        parts = lax.all_to_all(part.reshape(64, 8, 256), ("z", "y", "x"), 0, 0, tiled=True)
        env = jnp.sum(parts.astype(F32), axis=0).astype(BF)
    with jax.named_scope("gather_row"):
        env = jnp.broadcast_to(env, (2 * NZ * NY, 8, 256))
        env = lax.all_to_all(env, ("half",) + ROW, 0, 0, tiled=True)
    with jax.named_scope("gather_x"):
        across = [env] + [swap(env, ("x",), k) for k in range(1, NX)]
    with jax.named_scope("gather_e"):
        pieces = []
        for piece in across:
            pieces += [piece, swap(piece, ("e",), 1)]
    with jax.named_scope("final"):
        return final(me, by_rows, by_cols, pieces)


def solution(mesh):
    torus = Mesh(
        mesh.devices.reshape(2, NZ, NY, NX, NE), ("half", "z", "y", "x", "e")
    )
    in_specs = (
        P("half", ROW, COL, None),
        P("half", None, None, None, None),
        P("half", None, None),
        P("half", None),
        P(ALL, None, None),
    )
    return jax.shard_map(
        on_device, mesh=torus, in_specs=in_specs, out_specs=P(ALL, None, None), check_vma=False
    )
```

```python
import jax
import jax.numpy as jnp
from jax import lax
from jax.experimental import pallas as pl
from jax.experimental.pallas import tpu as pltpu
from jax.sharding import Mesh
from jax.sharding import PartitionSpec as P

BF = jnp.bfloat16
F32 = jnp.float32
NZ, NY, NX, NE = 8, 2, 4, 2
NF, NL = 2, 4
COL = ("x", "e")
ROW = ("far", "near", "y")
ALL = ("half",) + ROW + COL
MIXED_ROW = ("near", "far", "y")
MIXED_ALL = COL + ("y", "near", "far")
VMEM = pl.BlockSpec(memory_space=pltpu.VMEM)
SMEM = pl.BlockSpec(memory_space=pltpu.SMEM)
HBM = pl.BlockSpec(memory_space=pltpu.HBM)


def vmem(mebibytes):
    return pltpu.CompilerParams(vmem_limit_bytes=mebibytes << 20)


def dot(a, b, ca, cb):
    return lax.dot_general(a, b, (((ca,), (cb,)), ((), ())), preferred_element_type=F32)


def swap(value, axes, offset):
    peers = lax.axis_size(axes)
    return lax.ppermute(value, axes, [(i, i ^ offset) for i in range(peers)])


def terms_kernel(me, site, leg, table, *refs):
    blocks, (out_ref, ops, whole, inner, acc, arrived) = refs[: NX * NE], refs[NX * NE :]
    sites, terms, rows = ops.shape[1], leg.shape[0], whole.shape[0]
    fetch = [
        [pltpu.make_async_copy(table.at[w, s], ops.at[w, s], arrived.at[w, s]) for s in range(sites)]
        for w in range(2)
    ]
    for copy in fetch[1] + fetch[0]:
        copy.start()
    col = me[1] * NE + me[0]
    for k, ref in enumerate(blocks):
        for a in range(rows):
            whole[a, col ^ k] = ref[a]

    def any_term(test):
        found = test(0)
        for term in range(1, terms):
            found = found | test(term)
        return found

    @pl.when(any_term(lambda term: leg[term] == 0))
    def _():
        for a in range(rows):
            inner[sites, a] = whole[a].reshape(512, 512)

    for s in range(sites):
        fetch[1][s].wait()

        @pl.when(any_term(lambda term: (leg[term] != 0) & (site[term, 1] == s)))
        def _():
            for a in range(rows):
                inner[s, a] = dot(whole[a].reshape(512, 512), ops[1, s], 1, 1).astype(BF)

    for copy in fetch[0]:
        copy.wait()
    for term in range(terms):
        code = leg[term]
        held = jnp.where(code == 0, sites, site[term, 1])

        @pl.when(code != 1)
        def _():
            left = ops[0, site[term, 0]]
            for a in range(rows):
                part = dot(left, inner[held, a], 1, 0)
                acc[a] = part if term == 0 else acc[a] + part

        @pl.when(code == 1)
        def _():
            for a in range(rows):
                part = inner[held, a].astype(F32)
                acc[a] = part if term == 0 else acc[a] + part

    for a in range(rows):
        for x in range(NX):
            for e in range(NE):
                at = x * 128 + e * 64
                for y in range(NY):
                    block = acc[a, at : at + 64, y * 256 : (y + 1) * 256].astype(BF).reshape(NF, NL, 8, 256)
                    for far in range(NF):
                        out_ref[x, a // 2, y, :, far, a % 2, e] = block[far]


def apply_terms(me, site, leg, table, arrived):
    sites = table.shape[1]
    return pl.pallas_call(
        terms_kernel,
        out_shape=jax.ShapeDtypeStruct((NX, NE, NY, NL, NF, 2, NE, 8, 256), BF),
        in_specs=[SMEM] * 3 + [HBM] + [VMEM] * (NX * NE),
        out_specs=VMEM,
        scratch_shapes=[
            pltpu.VMEM((2, sites, 512, 512), BF),
            pltpu.VMEM((4, NX * NE, 64, 512), BF),
            pltpu.VMEM((sites + 1, 4, 512, 512), BF),
            pltpu.VMEM((4, 512, 512), F32),
            pltpu.SemaphoreType.DMA((2, sites)),
        ],
        compiler_params=vmem(50),
        name="terms",
    )(me, site, leg, table, *arrived)


def turn_kernel(in_ref, out_ref):
    out_ref[...] = jnp.swapaxes(in_ref[...], 0, 1)


def turned(value):
    peers, rows, depth, lanes = value.shape

    def place(i):
        near, far, y = i // (NF * NY), i // NY % NF, i % NY
        return 0, (far * NL + near) * NY + y, 0

    return pl.pallas_call(
        turn_kernel,
        out_shape=jax.ShapeDtypeStruct((depth, peers * rows, lanes), BF),
        grid=(peers,),
        in_specs=[pl.BlockSpec((None, rows, depth, lanes), lambda i: (i, 0, 0, 0))],
        out_specs=pl.BlockSpec((depth, rows, lanes), place),
        compiler_params=vmem(50),
        name="turn",
    )(value)


def gram_kernel(me, s_ref, own_ref, other_ref, out_ref, acc):
    e = me[0]
    first = True
    for which, c_ref in enumerate((own_ref, other_ref)):
        block = s_ref[:, :, e if which == 0 else 1 - e]
        block = jnp.swapaxes(block.reshape(256, 8, 256), 0, 1)
        for s in range(8):
            part = dot(block[s], c_ref[s], 1, 1)
            acc[...] = part if first else acc[...] + part
            first = False
    for z in range(NZ):
        for x in range(NX):
            at = (z * NX + x) * 8
            for y in range(NY):
                out_ref[z, y, x] = acc[at : at + 8, y * 256 : (y + 1) * 256].astype(BF)


def gram(me, summed, own, other):
    return pl.pallas_call(
        gram_kernel,
        out_shape=jax.ShapeDtypeStruct((NZ, NY, NX, 8, 256), BF),
        in_specs=[SMEM, VMEM, VMEM, VMEM],
        out_specs=VMEM,
        scratch_shapes=[pltpu.VMEM((256, 512), F32)],
        compiler_params=vmem(50),
        name="gram",
    )(me, summed, own, other)


def final_kernel(me, rows_ref, cols_ref, *refs):
    pieces, (out_ref, env, acc) = refs[: NX * NE], refs[-3:]
    e, x = me[0], me[1]
    for i, ref in enumerate(pieces):
        ke, kx = i % NE, i // NE
        block = (e ^ ke) * 32 + (x ^ kx)
        for half in range(2):
            for z in range(NZ):
                for y in range(NY):
                    env[half, y, block + z * NX] = ref[(half * NZ + z) * NY + y]
    for part in range(2):
        at = slice(part * 256, part * 256 + 256)
        one = env[0, part].reshape(512, 256)
        for c in range(2):
            acc[c, at, :] = dot(one, rows_ref[c], 0, 0)
    for part in range(2):
        at = slice(part * 256, part * 256 + 256)
        two = env[1, part].reshape(512, 256)
        for c in range(2):
            out_ref[c, :, at] = (acc[c, :, at] + dot(cols_ref[c], two, 1, 0)).astype(BF)


def final(me, by_rows, by_cols, pieces):
    return pl.pallas_call(
        final_kernel,
        out_shape=jax.ShapeDtypeStruct((2, 512, 512), BF),
        in_specs=[SMEM] + [VMEM] * (2 + NX * NE),
        out_specs=VMEM,
        scratch_shapes=[
            pltpu.VMEM((2, NY, 64, 8, 256), BF),
            pltpu.VMEM((2, 512, 512), F32),
        ],
        compiler_params=vmem(50),
        name="final",
    )(me, by_rows, by_cols, *pieces)


def reordered(parent):
    wanted = jnp.arange(512).reshape(NF, NL, NY, NX, NE, NE, 2)
    wanted = wanted.transpose(5, 3, 4, 2, 1, 0, 6).reshape(512)
    pick = (jnp.arange(512)[:, None] == wanted[None, :]).astype(BF)
    by_rows = jnp.einsum("aq,cab->cqb", pick, parent, preferred_element_type=F32)
    by_cols = jnp.einsum("cab,bq->caq", parent, pick, preferred_element_type=F32)
    return by_rows.astype(BF), by_cols.astype(BF)


def on_device(children, operators, term_site, term_leg, parent):
    me = jnp.stack([lax.axis_index(a) for a in ("e", "x")]).astype(jnp.int32)
    child = children[0]
    with jax.named_scope("child_rows"):
        cut = child.reshape(32, NF, NL, 8, NY, 256).transpose(2, 1, 4, 0, 3, 5)
        cut = cut.reshape(NZ * NY, 32 * 8, 256)
        child_all = lax.all_to_all(cut, MIXED_ROW, 0, 0, tiled=True)
    with jax.named_scope("child_first_leg"):
        col = lax.axis_index(COL)
        blocks = child.reshape(NX * NE, 4, 64, 512)
        arrived = []
        for k in range(NX * NE):
            block = lax.dynamic_index_in_dim(blocks, col ^ k, 0, keepdims=False)
            arrived.append(swap(block, COL, k) if k else block)
    with jax.named_scope("terms"):
        summed = apply_terms(
            me, term_site[0], term_leg[0], operators[0], arrived
        )
    with jax.named_scope("summed_rows"):
        summed = lax.all_to_all(summed.reshape(128, 32, 256), MIXED_ALL, 0, 0, tiled=True)
    with jax.named_scope("turn"):
        own = turned(child_all.reshape(NZ * NY, 32, 8, 256))
        other = swap(own, ("e",), 1)
        by_rows, by_cols = reordered(parent)
    with jax.named_scope("gram"):
        part = gram(me, summed.reshape(128, 2, NE, 8, 256), own, other)
    with jax.named_scope("sum"):
        parts = lax.all_to_all(part.reshape(64, 8, 256), ROW + ("x",), 0, 0, tiled=True)
        env = jnp.sum(parts.astype(F32), axis=0).astype(BF)
    with jax.named_scope("gather_row"):
        env = jnp.broadcast_to(env, (2 * NZ * NY, 8, 256))
        env = lax.all_to_all(env, ("half",) + ROW, 0, 0, tiled=True)
    with jax.named_scope("gather_x"):
        across = [env] + [swap(env, ("x",), k) for k in range(1, NX)]
    with jax.named_scope("gather_e"):
        pieces = []
        for piece in across:
            pieces += [piece, swap(piece, ("e",), 1)]
    with jax.named_scope("final"):
        return final(me, by_rows, by_cols, pieces)


def solution(mesh):
    torus = Mesh(
        mesh.devices.reshape(2, NF, NL, NY, NX, NE), ALL
    )
    in_specs = (
        P("half", ROW, COL, None),
        P("half", None, None, None, None),
        P("half", None, None),
        P("half", None),
        P(ALL, None, None),
    )
    return jax.shard_map(
        on_device, mesh=torus, in_specs=in_specs, out_specs=P(ALL, None, None), check_vma=False
    )
```

```python
import jax
import jax.numpy as jnp
from jax import lax
from jax.experimental import pallas as pl
from jax.experimental.pallas import tpu as pltpu
from jax.sharding import Mesh
from jax.sharding import PartitionSpec as P

BF = jnp.bfloat16
F32 = jnp.float32
NZ, NY, NX, NE = 8, 2, 4, 2
COL = ("x", "e")
ROW = ("z", "y")
ROW_COL = ROW + COL
ALL = ("half",) + ROW_COL
VMEM = pl.BlockSpec(memory_space=pltpu.VMEM)
SMEM = pl.BlockSpec(memory_space=pltpu.SMEM)
HBM = pl.BlockSpec(memory_space=pltpu.HBM)


def vmem(mebibytes):
    return pltpu.CompilerParams(vmem_limit_bytes=mebibytes << 20)


def dot(a, b, ca, cb):
    return lax.dot_general(a, b, (((ca,), (cb,)), ((), ())), preferred_element_type=F32)


def swap(value, axes, offset):
    peers = lax.axis_size(axes)
    return lax.ppermute(value, axes, [(i, i ^ offset) for i in range(peers)])


def terms_kernel(me, site, leg, table, *refs):
    blocks, (out_ref, ops, whole, inner, acc, arrived) = refs[: NX * NE], refs[NX * NE :]
    sites, terms, rows = ops.shape[1], leg.shape[0], whole.shape[0]
    fetch = [
        [pltpu.make_async_copy(table.at[w, s], ops.at[w, s], arrived.at[w, s]) for s in range(sites)]
        for w in range(2)
    ]
    for copy in fetch[1] + fetch[0]:
        copy.start()
    col = me[1] * NE + me[0]
    for k, ref in enumerate(blocks):
        for a in range(rows):
            whole[a, col ^ k] = ref[a]

    def any_term(test):
        found = test(0)
        for term in range(1, terms):
            found = found | test(term)
        return found

    @pl.when(any_term(lambda term: leg[term] == 0))
    def _():
        for a in range(rows):
            inner[sites, a] = whole[a].reshape(512, 512)

    for s in range(sites):
        fetch[1][s].wait()

        @pl.when(any_term(lambda term: (leg[term] != 0) & (site[term, 1] == s)))
        def _():
            for a in range(rows):
                inner[s, a] = dot(whole[a].reshape(512, 512), ops[1, s], 1, 1).astype(BF)

    for copy in fetch[0]:
        copy.wait()
    for term in range(terms):
        code = leg[term]
        held = jnp.where(code == 0, sites, site[term, 1])

        @pl.when(code != 1)
        def _():
            left = ops[0, site[term, 0]]
            for a in range(rows):
                part = dot(left, inner[held, a], 1, 0)
                acc[a] = part if term == 0 else acc[a] + part

        @pl.when(code == 1)
        def _():
            for a in range(rows):
                part = inner[held, a].astype(F32)
                acc[a] = part if term == 0 else acc[a] + part

    for a in range(rows):
        for x in range(NX):
            for e in range(NE):
                at = x * 128 + e * 64
                for y in range(NY):
                    block = acc[a, at : at + 64, y * 256 : (y + 1) * 256]
                    out_ref[:, y, x, a // 2, a % 2, e] = block.astype(BF).reshape(NZ, 8, 256)


def apply_terms(me, site, leg, table, arrived):
    sites = table.shape[1]
    return pl.pallas_call(
        terms_kernel,
        out_shape=jax.ShapeDtypeStruct((NZ, NY, NX, NE, 2, NE, 8, 256), BF),
        in_specs=[SMEM] * 3 + [HBM] + [VMEM] * (NX * NE),
        out_specs=VMEM,
        scratch_shapes=[
            pltpu.VMEM((2, sites, 512, 512), BF),
            pltpu.VMEM((4, NX * NE, 64, 512), BF),
            pltpu.VMEM((sites + 1, 4, 512, 512), BF),
            pltpu.VMEM((4, 512, 512), F32),
            pltpu.SemaphoreType.DMA((2, sites)),
        ],
        compiler_params=vmem(50),
        name="terms",
    )(me, site, leg, table, *arrived)


def turn_kernel(in_ref, out_ref):
    out_ref[...] = jnp.swapaxes(in_ref[...], 0, 1)


def turned(value):
    rows, depth, lanes = value.shape
    step = 64
    return pl.pallas_call(
        turn_kernel,
        out_shape=jax.ShapeDtypeStruct((depth, rows, lanes), BF),
        grid=(rows // step,),
        in_specs=[pl.BlockSpec((step, depth, lanes), lambda i: (i, 0, 0))],
        out_specs=pl.BlockSpec((depth, step, lanes), lambda i: (0, i, 0)),
        compiler_params=vmem(50),
        name="turn",
    )(value)


def gram_kernel(me, s_ref, own_ref, other_ref, out_ref, acc):
    e = me[0]
    first = True
    for which, c_ref in enumerate((own_ref, other_ref)):
        block = s_ref[:, :, e if which == 0 else 1 - e]
        block = jnp.swapaxes(block.reshape(256, 8, 256), 0, 1)
        for s in range(8):
            part = dot(block[s], c_ref[s], 1, 1)
            acc[...] = part if first else acc[...] + part
            first = False
    for z in range(NZ):
        for x in range(NX):
            at = (z * NX + x) * 8
            for y in range(NY):
                out_ref[z, y, x] = acc[at : at + 8, y * 256 : (y + 1) * 256].astype(BF)


def gram(me, summed, own, other):
    return pl.pallas_call(
        gram_kernel,
        out_shape=jax.ShapeDtypeStruct((NZ, NY, NX, 8, 256), BF),
        in_specs=[SMEM, VMEM, VMEM, VMEM],
        out_specs=VMEM,
        scratch_shapes=[pltpu.VMEM((256, 512), F32)],
        compiler_params=vmem(50),
        name="gram",
    )(me, summed, own, other)


def final_kernel(me, rows_ref, cols_ref, *refs):
    pieces, (out_ref, env, acc) = refs[:NE], refs[-3:]
    e = me[0]
    for i, ref in enumerate(pieces):
        for half in range(2):
            for z in range(NZ):
                for y in range(NY):
                    for x in range(NX):
                        env[half, y, (e ^ i) * 32 + z * NX + x] = ref[((half * NZ + z) * NY + y) * NX + x]
    for part in range(2):
        at = slice(part * 256, part * 256 + 256)
        one = env[0, part].reshape(512, 256)
        for c in range(2):
            acc[c, at, :] = dot(one, rows_ref[c], 0, 0)
    for part in range(2):
        at = slice(part * 256, part * 256 + 256)
        two = env[1, part].reshape(512, 256)
        for c in range(2):
            out_ref[c, :, at] = (acc[c, :, at] + dot(cols_ref[c], two, 1, 0)).astype(BF)


def final(me, by_rows, by_cols, pieces):
    return pl.pallas_call(
        final_kernel,
        out_shape=jax.ShapeDtypeStruct((2, 512, 512), BF),
        in_specs=[SMEM] + [VMEM] * (2 + NE),
        out_specs=VMEM,
        scratch_shapes=[
            pltpu.VMEM((2, NY, 64, 8, 256), BF),
            pltpu.VMEM((2, 512, 512), F32),
        ],
        compiler_params=vmem(50),
        name="final",
    )(me, by_rows, by_cols, *pieces)


def reordered(parent):
    wanted = jnp.arange(512).reshape(128, NE, 2).swapaxes(0, 1).reshape(512)
    pick = (jnp.arange(512)[:, None] == wanted[None, :]).astype(BF)
    by_rows = jnp.einsum("aq,cab->cqb", pick, parent, preferred_element_type=F32)
    by_cols = jnp.einsum("cab,bq->caq", parent, pick, preferred_element_type=F32)
    return by_rows.astype(BF), by_cols.astype(BF)


def on_device(children, operators, term_site, term_leg, parent):
    me = jnp.stack([lax.axis_index(a) for a in ("e", "x")]).astype(jnp.int32)
    child = children[0]
    with jax.named_scope("child_rows"):
        cut = child.reshape(32, NZ, 8, NY, 256).transpose(1, 3, 0, 2, 4)
        cut = cut.reshape(NZ * NY, 32 * 8, 256)
        child_all = lax.all_to_all(cut, ROW, 0, 0, tiled=True)
    with jax.named_scope("child_first_leg"):
        col = lax.axis_index(COL)
        blocks = child.reshape(NX * NE, 4, 64, 512)
        arrived = []
        for k in range(NX * NE):
            block = lax.dynamic_index_in_dim(blocks, col ^ k, 0, keepdims=False)
            arrived.append(swap(block, COL, k) if k else block)
    with jax.named_scope("terms"):
        summed = apply_terms(
            me, term_site[0], term_leg[0], operators[0], arrived
        )
    with jax.named_scope("summed_rows"):
        summed = lax.all_to_all(summed.reshape(128, 32, 256), ROW_COL, 0, 0, tiled=True)
    with jax.named_scope("turn"):
        own = turned(child_all.reshape(512, 8, 256))
        other = swap(own, ("e",), 1)
        by_rows, by_cols = reordered(parent)
    with jax.named_scope("gram"):
        part = gram(me, summed.reshape(128, 2, NE, 8, 256), own, other)
    with jax.named_scope("sum"):
        parts = lax.all_to_all(part.reshape(64, 8, 256), ("z", "y", "x"), 0, 0, tiled=True)
        env = jnp.sum(parts.astype(F32), axis=0).astype(BF)
    with jax.named_scope("gather"):
        env = jnp.broadcast_to(env, (2 * NZ * NY * NX, 8, 256))
        env = lax.all_to_all(env, ("half",) + ROW + ("x",), 0, 0, tiled=True)
        pieces = [env, swap(env, ("e",), 1)]
    with jax.named_scope("final"):
        return final(me, by_rows, by_cols, pieces)


def solution(mesh):
    torus = Mesh(
        mesh.devices.reshape(2, NZ, NY, NX, NE), ("half", "z", "y", "x", "e")
    )
    in_specs = (
        P("half", ROW, COL, None),
        P("half", None, None, None, None),
        P("half", None, None),
        P("half", None),
        P(ALL, None, None),
    )
    return jax.shard_map(
        on_device, mesh=torus, in_specs=in_specs, out_specs=P(ALL, None, None), check_vma=False
    )
```

```python
import jax
import jax.numpy as jnp
from jax import lax
from jax.experimental import pallas as pl
from jax.experimental.pallas import tpu as pltpu
from jax.sharding import Mesh
from jax.sharding import PartitionSpec as P

BF = jnp.bfloat16
F32 = jnp.float32
NZ, NY, NX, NE = 8, 2, 4, 2
COL = ("x", "e")
ROW = ("z", "y")
ROW_COL = ROW + COL
ALL = ("half",) + ROW_COL
VMEM = pl.BlockSpec(memory_space=pltpu.VMEM)
SMEM = pl.BlockSpec(memory_space=pltpu.SMEM)
HBM = pl.BlockSpec(memory_space=pltpu.HBM)


def vmem(mebibytes):
    return pltpu.CompilerParams(vmem_limit_bytes=mebibytes << 20)


def dot(a, b, ca, cb):
    return lax.dot_general(a, b, (((ca,), (cb,)), ((), ())), preferred_element_type=F32)


def swap(value, axes, offset):
    peers = lax.axis_size(axes)
    return lax.ppermute(value, axes, [(i, i ^ offset) for i in range(peers)])


def cut_kernel(child, out, held, arrived, left):
    pieces = [(z, y) for z in range(NZ) for y in range(NY)]
    takes = [
        pltpu.make_async_copy(
            child.at[:, z * 8 : z * 8 + 8, y * 256 : y * 256 + 256], held.at[i], arrived.at[i]
        )
        for i, (z, y) in enumerate(pieces)
    ]
    gives = [pltpu.make_async_copy(held.at[i], out.at[i], left.at[i]) for i in range(len(pieces))]
    for take in takes:
        take.start()
    for take, give in zip(takes, gives):
        take.wait()
        give.start()
    for give in gives:
        give.wait()


def cut_for_row(child):
    peers = NZ * NY
    return pl.pallas_call(
        cut_kernel,
        out_shape=jax.ShapeDtypeStruct((peers, 32, 8, 256), BF),
        in_specs=[HBM],
        out_specs=HBM,
        scratch_shapes=[
            pltpu.VMEM((peers, 32, 8, 256), BF),
            pltpu.SemaphoreType.DMA((peers,)),
            pltpu.SemaphoreType.DMA((peers,)),
        ],
        compiler_params=vmem(60),
        name="cut",
    )(child)


def terms_kernel(me, site, leg, table, *refs):
    blocks, (out_ref, ops, whole, inner, acc, arrived) = refs[: NX * NE], refs[NX * NE :]
    sites, terms, rows = ops.shape[1], leg.shape[0], whole.shape[0]
    fetch = [
        [pltpu.make_async_copy(table.at[w, s], ops.at[w, s], arrived.at[w, s]) for s in range(sites)]
        for w in range(2)
    ]
    for copy in fetch[1] + fetch[0]:
        copy.start()
    col = me[1] * NE + me[0]
    for k, ref in enumerate(blocks):
        for a in range(rows):
            whole[a, col ^ k] = ref[a]

    def any_term(test):
        found = test(0)
        for term in range(1, terms):
            found = found | test(term)
        return found

    @pl.when(any_term(lambda term: leg[term] == 0))
    def _():
        for a in range(rows):
            inner[sites, a] = whole[a].reshape(512, 512)

    for s in range(sites):
        fetch[1][s].wait()

        @pl.when(any_term(lambda term: (leg[term] != 0) & (site[term, 1] == s)))
        def _():
            for a in range(rows):
                inner[s, a] = dot(whole[a].reshape(512, 512), ops[1, s], 1, 1).astype(BF)

    for copy in fetch[0]:
        copy.wait()
    for term in range(terms):
        code = leg[term]
        held = jnp.where(code == 0, sites, site[term, 1])

        @pl.when(code != 1)
        def _():
            left = ops[0, site[term, 0]]
            for a in range(rows):
                part = dot(left, inner[held, a], 1, 0)
                acc[a] = part if term == 0 else acc[a] + part

        @pl.when(code == 1)
        def _():
            for a in range(rows):
                part = inner[held, a].astype(F32)
                acc[a] = part if term == 0 else acc[a] + part

    for a in range(rows):
        for x in range(NX):
            for e in range(NE):
                at = x * 128 + e * 64
                for y in range(NY):
                    block = acc[a, at : at + 64, y * 256 : (y + 1) * 256]
                    out_ref[:, y, x, a // 2, a % 2, e] = block.astype(BF).reshape(NZ, 8, 256)


def apply_terms(me, site, leg, table, arrived):
    sites = table.shape[1]
    return pl.pallas_call(
        terms_kernel,
        out_shape=jax.ShapeDtypeStruct((NZ, NY, NX, NE, 2, NE, 8, 256), BF),
        in_specs=[SMEM] * 3 + [HBM] + [VMEM] * (NX * NE),
        out_specs=VMEM,
        scratch_shapes=[
            pltpu.VMEM((2, sites, 512, 512), BF),
            pltpu.VMEM((4, NX * NE, 64, 512), BF),
            pltpu.VMEM((sites + 1, 4, 512, 512), BF),
            pltpu.VMEM((4, 512, 512), F32),
            pltpu.SemaphoreType.DMA((2, sites)),
        ],
        compiler_params=vmem(50),
        name="terms",
    )(me, site, leg, table, *arrived)


def turn_kernel(in_ref, out_ref):
    out_ref[...] = jnp.swapaxes(in_ref[...], 0, 1)


def turned(value):
    rows, depth, lanes = value.shape
    step = 64
    return pl.pallas_call(
        turn_kernel,
        out_shape=jax.ShapeDtypeStruct((depth, rows, lanes), BF),
        grid=(rows // step,),
        in_specs=[pl.BlockSpec((step, depth, lanes), lambda i: (i, 0, 0))],
        out_specs=pl.BlockSpec((depth, step, lanes), lambda i: (0, i, 0)),
        compiler_params=vmem(50),
        name="turn",
    )(value)


def gram_kernel(me, s_ref, own_ref, other_ref, out_ref, acc):
    e = me[0]
    first = True
    for which, c_ref in enumerate((own_ref, other_ref)):
        block = s_ref[:, :, e if which == 0 else 1 - e]
        block = jnp.swapaxes(block.reshape(256, 8, 256), 0, 1)
        for s in range(8):
            part = dot(block[s], c_ref[s], 1, 1)
            acc[...] = part if first else acc[...] + part
            first = False
    for z in range(NZ):
        for x in range(NX):
            at = (z * NX + x) * 8
            for y in range(NY):
                out_ref[z, y, x] = acc[at : at + 8, y * 256 : (y + 1) * 256].astype(BF)


def gram(me, summed, own, other):
    return pl.pallas_call(
        gram_kernel,
        out_shape=jax.ShapeDtypeStruct((NZ, NY, NX, 8, 256), BF),
        in_specs=[SMEM, VMEM, VMEM, VMEM],
        out_specs=VMEM,
        scratch_shapes=[pltpu.VMEM((256, 512), F32)],
        compiler_params=vmem(50),
        name="gram",
    )(me, summed, own, other)


def final_kernel(me, rows_ref, cols_ref, *refs):
    pieces, (out_ref, env, acc) = refs[: NX * NE], refs[-3:]
    e, x = me[0], me[1]
    for i, ref in enumerate(pieces):
        ke, kx = i % NE, i // NE
        block = (e ^ ke) * 32 + (x ^ kx)
        for half in range(2):
            for z in range(NZ):
                for y in range(NY):
                    env[half, y, block + z * NX] = ref[(half * NZ + z) * NY + y]
    for part in range(2):
        at = slice(part * 256, part * 256 + 256)
        one = env[0, part].reshape(512, 256)
        for c in range(2):
            acc[c, at, :] = dot(one, rows_ref[c], 0, 0)
    for part in range(2):
        at = slice(part * 256, part * 256 + 256)
        two = env[1, part].reshape(512, 256)
        for c in range(2):
            out_ref[c, :, at] = (acc[c, :, at] + dot(cols_ref[c], two, 1, 0)).astype(BF)


def final(me, by_rows, by_cols, pieces):
    return pl.pallas_call(
        final_kernel,
        out_shape=jax.ShapeDtypeStruct((2, 512, 512), BF),
        in_specs=[SMEM] + [VMEM] * (2 + NX * NE),
        out_specs=VMEM,
        scratch_shapes=[
            pltpu.VMEM((2, NY, 64, 8, 256), BF),
            pltpu.VMEM((2, 512, 512), F32),
        ],
        compiler_params=vmem(50),
        name="final",
    )(me, by_rows, by_cols, *pieces)


def reordered(parent):
    wanted = jnp.arange(512).reshape(128, NE, 2).swapaxes(0, 1).reshape(512)
    pick = (jnp.arange(512)[:, None] == wanted[None, :]).astype(BF)
    by_rows = jnp.einsum("aq,cab->cqb", pick, parent, preferred_element_type=F32)
    by_cols = jnp.einsum("cab,bq->caq", parent, pick, preferred_element_type=F32)
    return by_rows.astype(BF), by_cols.astype(BF)


def on_device(children, operators, term_site, term_leg, parent):
    me = jnp.stack([lax.axis_index(a) for a in ("e", "x")]).astype(jnp.int32)
    child = children[0]
    with jax.named_scope("child_rows"):
        cut = cut_for_row(child).reshape(NZ * NY, 32 * 8, 256)
        child_all = lax.all_to_all(cut, ROW, 0, 0, tiled=True)
    with jax.named_scope("child_first_leg"):
        col = lax.axis_index(COL)
        blocks = child.reshape(NX * NE, 4, 64, 512)
        arrived = []
        for k in range(NX * NE):
            block = lax.dynamic_index_in_dim(blocks, col ^ k, 0, keepdims=False)
            arrived.append(swap(block, COL, k) if k else block)
    with jax.named_scope("terms"):
        summed = apply_terms(
            me, term_site[0], term_leg[0], operators[0], arrived
        )
    with jax.named_scope("summed_rows"):
        summed = lax.all_to_all(summed.reshape(128, 32, 256), ROW_COL, 0, 0, tiled=True)
    with jax.named_scope("turn"):
        own = turned(child_all.reshape(512, 8, 256))
        other = swap(own, ("e",), 1)
        by_rows, by_cols = reordered(parent)
    with jax.named_scope("gram"):
        part = gram(me, summed.reshape(128, 2, NE, 8, 256), own, other)
    with jax.named_scope("sum"):
        parts = lax.all_to_all(part.reshape(64, 8, 256), ("z", "y", "x"), 0, 0, tiled=True)
        env = jnp.sum(parts.astype(F32), axis=0).astype(BF)
    with jax.named_scope("gather_row"):
        env = jnp.broadcast_to(env, (2 * NZ * NY, 8, 256))
        env = lax.all_to_all(env, ("half",) + ROW, 0, 0, tiled=True)
    with jax.named_scope("gather_x"):
        far = swap(env, ("x",), 2)
        across = [env, swap(env, ("x",), 1), far, swap(env, ("x",), 3)]
    with jax.named_scope("gather_e"):
        pieces = []
        for piece in across:
            pieces += [piece, swap(piece, ("e",), 1)]
    with jax.named_scope("final"):
        return final(me, by_rows, by_cols, pieces)


def solution(mesh):
    torus = Mesh(
        mesh.devices.reshape(2, NZ, NY, NX, NE), ("half", "z", "y", "x", "e")
    )
    in_specs = (
        P("half", ROW, COL, None),
        P("half", None, None, None, None),
        P("half", None, None),
        P("half", None),
        P(ALL, None, None),
    )
    return jax.shard_map(
        on_device, mesh=torus, in_specs=in_specs, out_specs=P(ALL, None, None), check_vma=False
    )
```

```python
import jax
import jax.numpy as jnp
from jax import lax
from jax.experimental import pallas as pl
from jax.experimental.pallas import tpu as pltpu
from jax.sharding import Mesh
from jax.sharding import PartitionSpec as P

BF = jnp.bfloat16
F32 = jnp.float32
NZ, NY, NX, NE = 8, 2, 4, 2
COL = ("x", "e")
ROW = ("z", "y")
ROW_COL = ROW + COL
ALL = ("half",) + ROW_COL
VMEM = pl.BlockSpec(memory_space=pltpu.VMEM)
SMEM = pl.BlockSpec(memory_space=pltpu.SMEM)
HBM = pl.BlockSpec(memory_space=pltpu.HBM)


def vmem(mebibytes):
    return pltpu.CompilerParams(vmem_limit_bytes=mebibytes << 20)


def dot(a, b, ca, cb):
    return lax.dot_general(a, b, (((ca,), (cb,)), ((), ())), preferred_element_type=F32)


def swap(value, axes, offset):
    peers = lax.axis_size(axes)
    return lax.ppermute(value, axes, [(i, i ^ offset) for i in range(peers)])


def cut_kernel(child, out, held, arrived, left):
    pieces = [(z, y) for z in range(NZ) for y in range(NY)]
    takes = [
        pltpu.make_async_copy(
            child.at[:, z * 8 : z * 8 + 8, y * 256 : y * 256 + 256], held.at[i], arrived.at[i]
        )
        for i, (z, y) in enumerate(pieces)
    ]
    gives = [pltpu.make_async_copy(held.at[i], out.at[i], left.at[i]) for i in range(len(pieces))]
    for take in takes:
        take.start()
    for take, give in zip(takes, gives):
        take.wait()
        give.start()
    for give in gives:
        give.wait()


def cut_for_row(child):
    peers = NZ * NY
    return pl.pallas_call(
        cut_kernel,
        out_shape=jax.ShapeDtypeStruct((peers, 32, 8, 256), BF),
        in_specs=[HBM],
        out_specs=HBM,
        scratch_shapes=[
            pltpu.VMEM((peers, 32, 8, 256), BF),
            pltpu.SemaphoreType.DMA((peers,)),
            pltpu.SemaphoreType.DMA((peers,)),
        ],
        compiler_params=vmem(60),
        name="cut",
    )(child)


def terms_kernel(me, site, leg, table, *refs):
    blocks, (out_ref, ops, whole, inner, acc, arrived) = refs[: NX * NE], refs[NX * NE :]
    sites, terms, rows = ops.shape[1], leg.shape[0], whole.shape[0]
    fetch = [
        [pltpu.make_async_copy(table.at[w, s], ops.at[w, s], arrived.at[w, s]) for s in range(sites)]
        for w in range(2)
    ]
    for copy in fetch[1] + fetch[0]:
        copy.start()
    col = me[1] * NE + me[0]
    for k, ref in enumerate(blocks):
        for a in range(rows):
            whole[a, col ^ k] = ref[a]

    def any_term(test):
        found = test(0)
        for term in range(1, terms):
            found = found | test(term)
        return found

    @pl.when(any_term(lambda term: leg[term] == 0))
    def _():
        for a in range(rows):
            inner[sites, a] = whole[a].reshape(512, 512)

    for s in range(sites):
        fetch[1][s].wait()

        @pl.when(any_term(lambda term: (leg[term] != 0) & (site[term, 1] == s)))
        def _():
            for a in range(rows):
                inner[s, a] = dot(whole[a].reshape(512, 512), ops[1, s], 1, 1).astype(BF)

    for copy in fetch[0]:
        copy.wait()
    for term in range(terms):
        code = leg[term]
        held = jnp.where(code == 0, sites, site[term, 1])

        @pl.when(code != 1)
        def _():
            left = ops[0, site[term, 0]]
            for a in range(rows):
                part = dot(left, inner[held, a], 1, 0)
                acc[a] = part if term == 0 else acc[a] + part

        @pl.when(code == 1)
        def _():
            for a in range(rows):
                part = inner[held, a].astype(F32)
                acc[a] = part if term == 0 else acc[a] + part

    for a in range(rows):
        for x in range(NX):
            for e in range(NE):
                at = x * 128 + e * 64
                for y in range(NY):
                    block = acc[a, at : at + 64, y * 256 : (y + 1) * 256]
                    out_ref[:, y, x, a // 2, a % 2, e] = block.astype(BF).reshape(NZ, 8, 256)


def apply_terms(me, site, leg, table, arrived):
    sites = table.shape[1]
    return pl.pallas_call(
        terms_kernel,
        out_shape=jax.ShapeDtypeStruct((NZ, NY, NX, NE, 2, NE, 8, 256), BF),
        in_specs=[SMEM] * 3 + [HBM] + [VMEM] * (NX * NE),
        out_specs=VMEM,
        scratch_shapes=[
            pltpu.VMEM((2, sites, 512, 512), BF),
            pltpu.VMEM((4, NX * NE, 64, 512), BF),
            pltpu.VMEM((sites + 1, 4, 512, 512), BF),
            pltpu.VMEM((4, 512, 512), F32),
            pltpu.SemaphoreType.DMA((2, sites)),
        ],
        compiler_params=vmem(50),
        name="terms",
    )(me, site, leg, table, *arrived)


def turn_kernel(in_ref, out_ref):
    out_ref[...] = jnp.swapaxes(in_ref[...], 0, 1)


def turned(value):
    rows, depth, lanes = value.shape
    step = 64
    return pl.pallas_call(
        turn_kernel,
        out_shape=jax.ShapeDtypeStruct((depth, rows, lanes), BF),
        grid=(rows // step,),
        in_specs=[pl.BlockSpec((step, depth, lanes), lambda i: (i, 0, 0))],
        out_specs=pl.BlockSpec((depth, step, lanes), lambda i: (0, i, 0)),
        compiler_params=vmem(50),
        name="turn",
    )(value)


def gram_kernel(me, s_ref, own_ref, other_ref, out_ref, acc):
    e = me[0]
    first = True
    for which, c_ref in enumerate((own_ref, other_ref)):
        block = s_ref[:, :, e if which == 0 else 1 - e]
        block = jnp.swapaxes(block.reshape(256, 8, 256), 0, 1)
        for s in range(8):
            part = dot(block[s], c_ref[s], 1, 1)
            acc[...] = part if first else acc[...] + part
            first = False
    for z in range(NZ):
        for x in range(NX):
            at = (z * NX + x) * 8
            for y in range(NY):
                out_ref[z, y, x] = acc[at : at + 8, y * 256 : (y + 1) * 256].astype(BF)


def gram(me, summed, own, other):
    return pl.pallas_call(
        gram_kernel,
        out_shape=jax.ShapeDtypeStruct((NZ, NY, NX, 8, 256), BF),
        in_specs=[SMEM, VMEM, VMEM, VMEM],
        out_specs=VMEM,
        scratch_shapes=[pltpu.VMEM((256, 512), F32)],
        compiler_params=vmem(50),
        name="gram",
    )(me, summed, own, other)


def final_kernel(me, rows_ref, cols_ref, *refs):
    pieces, (out_ref, env, acc) = refs[: NX * NE], refs[-3:]
    e, x = me[0], me[1]
    for i, ref in enumerate(pieces):
        ke, kx = i % NE, i // NE
        block = (e ^ ke) * 32 + (x ^ kx)
        for half in range(2):
            for z in range(NZ):
                for y in range(NY):
                    env[half, y, block + z * NX] = ref[(z * 2 + half) * NY + y]
    for part in range(2):
        at = slice(part * 256, part * 256 + 256)
        one = env[0, part].reshape(512, 256)
        for c in range(2):
            acc[c, at, :] = dot(one, rows_ref[c], 0, 0)
    for part in range(2):
        at = slice(part * 256, part * 256 + 256)
        two = env[1, part].reshape(512, 256)
        for c in range(2):
            out_ref[c, :, at] = (acc[c, :, at] + dot(cols_ref[c], two, 1, 0)).astype(BF)


def final(me, by_rows, by_cols, pieces):
    return pl.pallas_call(
        final_kernel,
        out_shape=jax.ShapeDtypeStruct((2, 512, 512), BF),
        in_specs=[SMEM] + [VMEM] * (2 + NX * NE),
        out_specs=VMEM,
        scratch_shapes=[
            pltpu.VMEM((2, NY, 64, 8, 256), BF),
            pltpu.VMEM((2, 512, 512), F32),
        ],
        compiler_params=vmem(50),
        name="final",
    )(me, by_rows, by_cols, *pieces)


def reordered(parent):
    wanted = jnp.arange(512).reshape(128, NE, 2).swapaxes(0, 1).reshape(512)
    pick = (jnp.arange(512)[:, None] == wanted[None, :]).astype(BF)
    by_rows = jnp.einsum("aq,cab->cqb", pick, parent, preferred_element_type=F32)
    by_cols = jnp.einsum("cab,bq->caq", parent, pick, preferred_element_type=F32)
    return by_rows.astype(BF), by_cols.astype(BF)


def on_device(children, operators, term_site, term_leg, parent):
    me = jnp.stack([lax.axis_index(a) for a in ("e", "x")]).astype(jnp.int32)
    child = children[0]
    with jax.named_scope("child_rows"):
        cut = cut_for_row(child).reshape(NZ * NY, 32 * 8, 256)
        child_all = lax.all_to_all(cut, ROW, 0, 0, tiled=True)
    with jax.named_scope("child_first_leg"):
        col = lax.axis_index(COL)
        blocks = child.reshape(NX * NE, 4, 64, 512)
        arrived = []
        for k in range(NX * NE):
            block = lax.dynamic_index_in_dim(blocks, col ^ k, 0, keepdims=False)
            arrived.append(swap(block, COL, k) if k else block)
    with jax.named_scope("terms"):
        summed = apply_terms(
            me, term_site[0], term_leg[0], operators[0], arrived
        )
    with jax.named_scope("summed_rows"):
        summed = lax.all_to_all(summed.reshape(128, 32, 256), ROW_COL, 0, 0, tiled=True)
    with jax.named_scope("turn"):
        own = turned(child_all.reshape(512, 8, 256))
        other = swap(own, ("e",), 1)
        by_rows, by_cols = reordered(parent)
    with jax.named_scope("gram"):
        part = gram(me, summed.reshape(128, 2, NE, 8, 256), own, other)
    with jax.named_scope("sum"):
        parts = lax.all_to_all(part.reshape(64, 8, 256), ("z", "y", "x"), 0, 0, tiled=True)
        env = jnp.sum(parts.astype(F32), axis=0).astype(BF)
    with jax.named_scope("gather_row"):
        env = jnp.broadcast_to(env, (2 * NZ * NY, 8, 256))
        env = lax.all_to_all(env, ("z", "half", "y"), 0, 0, tiled=True)
    with jax.named_scope("gather_x"):
        far = swap(env, ("x",), 2)
        across = [env, swap(env, ("x",), 1), far, swap(env, ("x",), 3)]
    with jax.named_scope("gather_e"):
        pieces = []
        for piece in across:
            pieces += [piece, swap(piece, ("e",), 1)]
    with jax.named_scope("final"):
        return final(me, by_rows, by_cols, pieces)


def solution(mesh):
    torus = Mesh(
        mesh.devices.reshape(2, NZ, NY, NX, NE), ("half", "z", "y", "x", "e")
    )
    in_specs = (
        P("half", ROW, COL, None),
        P("half", None, None, None, None),
        P("half", None, None),
        P("half", None),
        P(ALL, None, None),
    )
    return jax.shard_map(
        on_device, mesh=torus, in_specs=in_specs, out_specs=P(ALL, None, None), check_vma=False
    )
```
